32 devices in a mesh: grp: 2 (over x), cand: 16 (over z, y, core).
Axes of the slice: x: 2, y: 2, z: 4, core: 2. Of those that a mesh axis runs over, the one named last changes fastest.
Arguments:
- prompt_key_rows: bfloat16 [256, 512], P(('grp', 'cand')), parts along dimension 0, may hold values from -6 to 6
- prompt_value_rows: bfloat16 [256, 512], P(('grp', 'cand')), parts along dimension 0, may hold values from -6 to 6
- queries: bfloat16 [4096, 4096], P(('grp', 'cand')), parts along dimension 0, may hold values from -6 to 6
- keys: bfloat16 [4096, 512], P(('grp', 'cand')), parts along dimension 0, may hold values from -6 to 6
- values: bfloat16 [4096, 512], P(('grp', 'cand')), parts along dimension 0, may hold values from -6 to 6
- output_gradient: bfloat16 [4096, 4096], P(('grp', 'cand')), parts along dimension 0, may hold values from -12 to 12
- lengths: int32 [32], P(('grp', 'cand')), parts along dimension 0, may hold values from 1 to 120, 640 in all
- prompt_visible_rows: int32 [32], P(('grp', 'cand')), parts along dimension 0, may hold values from 32 to 128
- query_gain: float32 [128], replicated, may hold values from 0.25 to 1.75
- key_norm_gain: float32 [128], replicated, may hold values from 0.25 to 1.75
- key_value_weight: bfloat16 [5120, 1024], P('cand'), may hold values from -0.25 to 0.25
Outputs:
- query_grad: bfloat16 [4096, 4096], P(('grp', 'cand')), parts along dimension 0
- key_grad: bfloat16 [4096, 512], P(('grp', 'cand')), parts along dimension 0
- value_grad: bfloat16 [4096, 512], P(('grp', 'cand')), parts along dimension 0
- prompt_hidden_grad: bfloat16 [256, 5120], P(('grp', 'cand')), parts along dimension 0
The draws below stay inside these ranges and needn't reach their ends.
There are 2 independent parts, one for each index of `grp`. The reference program is written for one: setup_inputs(seed, part) draws one part's arguments, and reference() takes and returns one part's arrays. A program takes and returns all parts, laid end to end along the dimension named above; an argument that names none is the same for every part. Nothing has to cross between parts.
Inputs may be any that keep to these rules, and one draw needn't show every extreme that they name: The first lengths[c] of candidate c's 128 slots hold its response, the rest are padding.
All inputs are finite; a program needn't handle non-finite values. No bound on the sum of `lengths` on one device may be relied on, other than what follows from the above.
Results may differ from the reference program's by a relative error of at most 0.0098.
Values may be sent and summed in bfloat16 or wider, within the bound.
A program may use at most 128 MiB of HBM per device.

```python
import math
import jax
import jax.numpy as jnp
import numpy as np
from jax import lax

MODEL_WIDTH = 5120
QUERY_HEADS = 32
KEY_VALUE_HEADS = 4
HEAD_WIDTH = 128
RESPONSE_SLOTS = 128
LONGEST = 120
MEAN_LEN = 40
PROMPT_ROWS = 128
CANDIDATE_COUNT = 16


def with_ends(drawn, key, least, top_value):
    place = [jax.random.randint(jax.random.fold_in(key, axis), (), 0, length) for axis, length in enumerate(drawn.shape)]
    longest = drawn.shape.index(max(drawn.shape))
    neighbour = place[:longest] + [(place[longest] + 1) % drawn.shape[longest]] + place[longest + 1:]
    return drawn.at[tuple(place)].set(least).at[tuple(neighbour)].set(top_value)


def steps_of(rng, extent, split, low, top_value):
    level = 1.0
    for position, blocks in split:
        heights = jax.random.uniform(jax.random.fold_in(jax.random.fold_in(rng, 6), position), (blocks,), jnp.float32, low / len(split), top_value / len(split))
        level = level * jnp.repeat(jnp.exp(heights), extent[position] // blocks).reshape((-1,) + (1,) * (len(extent) - 1 - position))
    return level


def split_up(amount, total, most, skew):
    loads = [(1 << 20) // math.isqrt(standing ** skew) + 1 for standing in range(2, amount + 1)]
    surplus, holding = total - most - (amount - 1), [1] * (amount - 1)
    while surplus > 0:
        free = [i for i in range(amount - 1) if holding[i] < most]
        pool, left = sum([loads[i] for i in free]), surplus
        for i in free:
            extra = min(most - holding[i], max(1, left * loads[i] // pool), surplus)
            holding[i] = holding[i] + extra
            surplus = surplus - extra
    return np.array([most] + holding)


def ragged(own_key, amount, total, limit, skew):
    if amount == 2:
        one = jax.random.randint(own_key, (), max(1, total - limit), min(limit, total - 1) + 1)
        return jnp.stack([one, total - one])
    sizes = jnp.asarray(split_up(amount, total, limit, skew), jnp.int32)
    couples = (amount - 1) // 2
    source_of, sink = sizes[1:1 + 2 * couples:2], sizes[2:2 + 2 * couples:2]
    room = jnp.minimum(source_of - 1, limit - sink)
    passed = jax.random.randint(jax.random.fold_in(own_key, 1), (couples,), 0, 1 << 20) % (room + 1)
    sizes = sizes.at[1:1 + 2 * couples:2].set(source_of - passed).at[2:2 + 2 * couples:2].set(sink + passed)
    return sizes[jax.random.permutation(jax.random.fold_in(own_key, 2), amount)]


def scatter_about(own_key, shape, spread, bound, cuts=(), held_as=jnp.bfloat16):
    level = steps_of(own_key, shape, cuts, -0.22, 0.18) if cuts else 1.0
    result = jax.random.normal(own_key, shape, jnp.float32) * spread * level
    return jnp.minimum(jnp.maximum(result, -bound), bound).astype(held_as)


def setup_inputs(seed: int = 0, part: int = 0) -> dict:
    splits = jax.random.split(jax.random.key(seed), 12)
    part_keys = jax.random.split(jax.random.fold_in(splits[11], part), 12)
    return {
        "prompt_key_rows": scatter_about(part_keys[0], (PROMPT_ROWS, KEY_VALUE_HEADS * HEAD_WIDTH), 1.0, 6.0, ((0, 16),)),
        "prompt_value_rows": scatter_about(part_keys[1], (PROMPT_ROWS, KEY_VALUE_HEADS * HEAD_WIDTH), 1.0, 6.0, ((0, 16),)),
        "queries": scatter_about(part_keys[2], (CANDIDATE_COUNT * RESPONSE_SLOTS, QUERY_HEADS * HEAD_WIDTH), 1.0, 6.0, ((0, 16),)),
        "keys": scatter_about(part_keys[3], (CANDIDATE_COUNT * RESPONSE_SLOTS, KEY_VALUE_HEADS * HEAD_WIDTH), 1.0, 6.0, ((0, 16),)),
        "values": scatter_about(part_keys[4], (CANDIDATE_COUNT * RESPONSE_SLOTS, KEY_VALUE_HEADS * HEAD_WIDTH), 1.0, 6.0, ((0, 16),)),
        "output_gradient": scatter_about(part_keys[5], (CANDIDATE_COUNT * RESPONSE_SLOTS, QUERY_HEADS * HEAD_WIDTH), 2.0, 12.0, ((0, 16),)),
        "lengths": ragged(part_keys[6], CANDIDATE_COUNT, MEAN_LEN * CANDIDATE_COUNT, LONGEST, 2).astype(jnp.int32),
        "prompt_visible_rows": with_ends(jax.random.randint(part_keys[7], (CANDIDATE_COUNT,), PROMPT_ROWS // 4, PROMPT_ROWS + 1), jax.random.fold_in(part_keys[7], 1), PROMPT_ROWS // 4, PROMPT_ROWS).astype(jnp.int32),
        "query_gain": jnp.clip(1.0 + 0.15 * jax.random.normal(splits[8], (HEAD_WIDTH,), jnp.float32), 0.25, 1.75),
        "key_norm_gain": jnp.clip(1.0 + 0.15 * jax.random.normal(splits[9], (HEAD_WIDTH,), jnp.float32), 0.25, 1.75),
        "key_value_weight": scatter_about(splits[10], (MODEL_WIDTH, 2 * KEY_VALUE_HEADS * HEAD_WIDTH), (KEY_VALUE_HEADS * HEAD_WIDTH) ** -0.5, 0.25, ((0, 16),)),
    }


epsilon = 1e-06

def head_norm_forward(raw, gain, heads):
    count = raw.shape[0]
    inputs = raw.astype(jnp.float32).reshape(count, heads, -1)
    factor = lax.rsqrt(lax.optimization_barrier(jnp.mean(inputs * inputs, axis=-1, keepdims=True)) + epsilon)
    normed = (inputs * factor * gain).reshape(count, -1).astype(jnp.bfloat16)
    return (inputs, factor, normed)

def norm_backward(inputs, factor, gain, upstream):
    count = inputs.shape[0]
    scaled = upstream.reshape(inputs.shape) * gain
    inner = lax.optimization_barrier(jnp.mean(scaled * inputs, axis=-1, keepdims=True))
    return (factor * scaled - inputs * (factor * factor * factor) * inner).reshape(count, -1)

def contract_rows(left, right):
    return lax.dot_general(left, right, (((0,), (0,)), ((), ())), preferred_element_type=jnp.float32)

def attend(normed_q, all_keys, all_values, masked_grad, visible, head_dim):
    count = normed_q.shape[0]
    total = all_keys.shape[0]
    kv_heads = all_keys.shape[1] // head_dim
    group = normed_q.shape[1] // (kv_heads * head_dim)
    scale = head_dim ** (-0.5)
    weight_mask = visible.astype(jnp.float32)[:, None, :]
    q_parts, k_parts, v_parts = ([], [], [])
    for head in range(kv_heads):
        width = group * head_dim
        q_block = normed_q[:, head * width:(head + 1) * width].reshape(count * group, head_dim)
        g_block = masked_grad[:, head * width:(head + 1) * width].reshape(count * group, head_dim)
        k_block = all_keys[:, head * head_dim:(head + 1) * head_dim]
        v_block = all_values[:, head * head_dim:(head + 1) * head_dim]
        scores = jnp.dot(q_block, k_block.T, preferred_element_type=jnp.float32).reshape(count, group, total) * scale
        expo = jnp.exp(scores) * weight_mask
        probs = expo / lax.optimization_barrier(jnp.sum(expo, axis=-1, keepdims=True))
        probs_low = probs.astype(jnp.bfloat16).reshape(count * group, total)
        v_parts.append(contract_rows(probs_low, g_block))
        dprobs = jnp.dot(g_block, v_block.T, preferred_element_type=jnp.float32).reshape(count, group, total)
        delta = lax.optimization_barrier(jnp.sum(probs * dprobs, axis=-1, keepdims=True))
        dscore = (probs * (dprobs - delta) * scale).astype(jnp.bfloat16).reshape(count * group, total)
        q_parts.append(jnp.dot(dscore, k_block, preferred_element_type=jnp.float32).reshape(count, width))
        k_parts.append(contract_rows(dscore, q_block))
    return (jnp.concatenate(q_parts, axis=1), jnp.concatenate(k_parts, axis=1), jnp.concatenate(v_parts, axis=1))

def reference(prompt_key_rows, prompt_value_rows, queries, keys, values, output_gradient, lengths, prompt_visible_rows, query_gain, key_norm_gain, key_value_weight):
    prompt_norm_inputs, prompt_norm_factor, prompt_after_norm = head_norm_forward(prompt_key_rows, key_norm_gain, KEY_VALUE_HEADS)
    prompt_index = jnp.arange(PROMPT_ROWS, dtype=jnp.int32)
    slot_index = jnp.arange(RESPONSE_SLOTS, dtype=jnp.int32)
    causal = slot_index[None, :] <= slot_index[:, None]

    def one_candidate(carry, item_list):
        q_raw, key_before_norm, v_raw, g_raw, length, seen = item_list
        q_inputs, q_factor, q_normed = head_norm_forward(q_raw, query_gain, QUERY_HEADS)
        key_norm_inputs, key_norm_factor, key_after_norm = head_norm_forward(key_before_norm, key_norm_gain, KEY_VALUE_HEADS)
        masked_grad = jnp.where((slot_index < length)[:, None], g_raw, jnp.zeros_like(g_raw))
        prompt_visible = jnp.broadcast_to((prompt_index < seen)[None, :], (RESPONSE_SLOTS, PROMPT_ROWS))
        visible = jnp.concatenate([prompt_visible, causal], axis=1)
        all_keys = jnp.concatenate([prompt_after_norm, key_after_norm], axis=0)
        all_values = jnp.concatenate([prompt_value_rows, v_raw], axis=0)
        dq_n, dk_n, dv_n = attend(q_normed, all_keys, all_values, masked_grad, visible, HEAD_WIDTH)
        q_out = norm_backward(q_inputs, q_factor, query_gain, dq_n).astype(jnp.bfloat16)
        k_out = norm_backward(key_norm_inputs, key_norm_factor, key_norm_gain, dk_n[PROMPT_ROWS:]).astype(jnp.bfloat16)
        v_out = dv_n[PROMPT_ROWS:].astype(jnp.bfloat16)
        return ((carry[0] + dk_n[:PROMPT_ROWS], carry[1] + dv_n[:PROMPT_ROWS]), (q_out, k_out, v_out))
    zero_filled = jnp.zeros((PROMPT_ROWS, KEY_VALUE_HEADS * HEAD_WIDTH), jnp.float32)
    item_list = (queries.reshape(CANDIDATE_COUNT, RESPONSE_SLOTS, QUERY_HEADS * HEAD_WIDTH), keys.reshape(CANDIDATE_COUNT, RESPONSE_SLOTS, KEY_VALUE_HEADS * HEAD_WIDTH), values.reshape(CANDIDATE_COUNT, RESPONSE_SLOTS, KEY_VALUE_HEADS * HEAD_WIDTH), output_gradient.reshape(CANDIDATE_COUNT, RESPONSE_SLOTS, QUERY_HEADS * HEAD_WIDTH), lengths, prompt_visible_rows)
    sums, output_list = lax.scan(one_candidate, (zero_filled, zero_filled), item_list)
    prompt_dk = norm_backward(prompt_norm_inputs, prompt_norm_factor, key_norm_gain, sums[0]).astype(jnp.bfloat16)
    prompt_grads = jnp.concatenate([prompt_dk, sums[1].astype(jnp.bfloat16)], axis=1)
    hidden_state = lax.dot_general(prompt_grads, key_value_weight, (((1,), (1,)), ((), ())), preferred_element_type=jnp.float32).astype(jnp.bfloat16)
    return (output_list[0].reshape(CANDIDATE_COUNT * RESPONSE_SLOTS, QUERY_HEADS * HEAD_WIDTH), output_list[1].reshape(CANDIDATE_COUNT * RESPONSE_SLOTS, KEY_VALUE_HEADS * HEAD_WIDTH), output_list[2].reshape(CANDIDATE_COUNT * RESPONSE_SLOTS, KEY_VALUE_HEADS * HEAD_WIDTH), hidden_state)
```

```python
import functools
import math

import jax
import jax.numpy as jnp
from jax import lax
from jax.experimental import pallas as pl
from jax.experimental.pallas import tpu as pltpu
from jax.sharding import PartitionSpec as P

EPS = 1e-06
F32 = jnp.float32
BF16 = jnp.bfloat16


def dot_nt(a, b):
    return lax.dot_general(a, b, (((1,), (1,)), ((), ())), preferred_element_type=F32)


def dot_nn(a, b):
    return lax.dot_general(a, b, (((1,), (0,)), ((), ())), preferred_element_type=F32)


def kernel(
    n,
    len_ref,
    seen_ref,
    gq_ref,
    gk_ref,
    pk_hbm,
    pv_hbm,
    q_hbm,
    k_hbm,
    v_hbm,
    g_hbm,
    w_hbm,
    qo_hbm,
    ko_ref,
    vo_ref,
    ho_ref,
    pkv,
    qv,
    kv,
    vv,
    gv,
    wv,
    mask,
    dsv,
    xcv,
    kgt,
    acc,
    qo,
    rs_src,
    rs_dst,
    ag,
    hs_src,
    hs_dst,
    own_sem,
    in_sem,
    out_sem,
    pg_send,
    pg_recv,
    rs_send,
    rs_recv,
    ag_send,
    ag_recv,
    hs_send,
    hs_recv,
):
    me = lax.axis_index("cand")
    slots, q_width = qv.shape
    kv_heads = rs_src.shape[0]
    per = pkv.shape[2]
    dim = gq_ref.shape[0]
    prompt = n * per
    total = prompt + slots
    group = q_width // (kv_heads * dim)
    wide = 2 if group % 2 == 0 else 1
    pairs = group // wide
    lanes = wide * slots
    scale = dim ** (-0.5)

    own = [
        pltpu.make_async_copy(pk_hbm, pkv.at[me, 0], own_sem.at[0]),
        pltpu.make_async_copy(pv_hbm, pkv.at[me, 1], own_sem.at[1]),
    ]
    loads = [
        pltpu.make_async_copy(src, dst, in_sem.at[i])
        for i, (src, dst) in enumerate(
            ((k_hbm, kv), (v_hbm, vv), (q_hbm, qv), (g_hbm, gv), (w_hbm, wv))
        )
    ]
    for copy in own + loads:
        copy.start()

    barrier = pltpu.get_barrier_semaphore()

    def greet(step, _):
        peer = lax.rem(me + step, n)
        pl.semaphore_signal(
            barrier, inc=1, device_id={"cand": peer}, device_id_type=pl.DeviceIdType.MESH
        )
        return 0

    lax.fori_loop(1, n, greet, 0)
    pl.semaphore_wait(barrier, n - 1)

    def send_all(copy_of):
        def body(step, _):
            copy_of(lax.rem(me + step, n)).start()
            return 0

        lax.fori_loop(1, n, body, 0)

    def remote(src, dst, send, recv):
        def copy_of(peer):
            return pltpu.make_async_remote_copy(
                src_ref=src(peer),
                dst_ref=dst,
                send_sem=send,
                recv_sem=recv,
                device_id={"cand": peer},
                device_id_type=pl.DeviceIdType.MESH,
            )

        return copy_of

    def drain(buffer, sem):
        part = buffer.at[pl.ds(0, n - 1)]
        pltpu.make_async_copy(part, part, sem).wait()

    for copy in own:
        copy.wait()
    send_all(remote(lambda peer: pkv.at[me], pkv.at[me], pg_send, pg_recv))

    gq = gq_ref[...].reshape(1, dim)
    gk = gk_ref[...].reshape(1, dim)
    both = gq * gk
    row = lax.broadcasted_iota(jnp.int32, (slots, dim), 0)
    live = (row < len_ref[0]).astype(F32).astype(BF16)
    key = lax.broadcasted_iota(jnp.int32, (prompt, slots), 0)
    seen = (key < seen_ref[0]).astype(F32)
    slot_j = lax.broadcasted_iota(jnp.int32, (slots, slots), 0)
    slot_i = lax.broadcasted_iota(jnp.int32, (slots, slots), 1)
    causal = (slot_j <= slot_i).astype(F32)
    for b in range(wide):
        mask[:prompt, b * slots : (b + 1) * slots] = seen
        mask[prompt:, b * slots : (b + 1) * slots] = causal
    eye_r = lax.broadcasted_iota(jnp.int32, (dim, dim), 0)
    eye_c = lax.broadcasted_iota(jnp.int32, (dim, dim), 1)
    eye = (eye_r == eye_c).astype(F32).astype(BF16)

    def head_lanes(head):
        return pl.ds(pl.multiple_of(head * dim, dim), dim)

    def key_factor(x):
        return lax.rsqrt(jnp.mean(x * x, axis=-1, keepdims=True) + EPS)

    for copy in loads:
        copy.wait()
    drain(pkv, pg_recv)

    def forward(h, _):
        raw = jnp.concatenate(
            [
                pkv[:, 0, :, head_lanes(h)].astype(F32).reshape(prompt, dim),
                kv[:, head_lanes(h)].astype(F32),
            ],
            axis=0,
        )
        kg32 = raw * key_factor(raw) * both
        kgt[h] = kg32.T.astype(BF16)
        left = jnp.concatenate([kg32.astype(BF16), eye], axis=0)
        val = jnp.concatenate(
            [
                pkv[:, 1, :, head_lanes(h)].astype(F32).reshape(prompt, dim).astype(BF16),
                vv[:, head_lanes(h)],
            ],
            axis=0,
        )
        dk = dv = None
        for b in range(pairs):
            heads = [h * group + b * wide + a for a in range(wide)]
            x2 = jnp.concatenate([qv[:, head_lanes(a)] for a in heads], axis=0)
            g2 = jnp.concatenate([gv[:, head_lanes(a)] * live for a in heads], axis=0)
            both_t = dot_nt(left, x2)
            x_t = both_t[total:]
            r = lax.rsqrt(jnp.mean(x_t * x_t, axis=0, keepdims=True) + EPS)
            z = both_t[:total] * (r * (scale * math.log2(math.e)))
            e = jnp.exp2(z) * mask[...]
            dp = dot_nt(val, g2)
            inv = 1.0 / jnp.sum(e, axis=0, keepdims=True)
            p = e * inv
            delta = jnp.sum(p * dp, axis=0, keepdims=True)
            ds = p * (dp - delta)
            inner = jnp.sum(ds * z, axis=0, keepdims=True)
            xcv[h, b] = x_t * (r * r * inner * (math.log(2.0) / dim))
            ds = (ds * (r * scale)).astype(BF16)
            dsv[h, b] = ds
            dv_b = dot_nn(p.astype(BF16), g2)
            dk_b = dot_nn(ds, x2)
            dv = dv_b if dv is None else dv + dv_b
            dk = dk_b if dk is None else dk + dk_b
        rs_src[h, :, :, :dim] = dk[:prompt].reshape(n, per, dim).astype(BF16)
        rs_src[h, :, :, dim:] = dv[:prompt].reshape(n, per, dim).astype(BF16)
        send_all(
            remote(
                lambda peer: rs_src.at[h, peer],
                rs_dst.at[h, me],
                rs_send.at[h],
                rs_recv.at[h],
            )
        )
        rs_dst[h, me] = rs_src[h, me]
        acc[h, :, :dim] = dk[prompt:]
        acc[h, :, dim:] = dv[prompt:]
        return 0

    lax.fori_loop(0, kv_heads, forward, 0)

    def query_side(h, _):
        for b in range(pairs):
            dx = dot_nn(kgt[h], dsv[h, b]) - xcv[h, b]
            for a in range(wide):
                head = h * group + b * wide + a
                qo[:, head_lanes(head)] = dx[:, a * slots : (a + 1) * slots].T.astype(BF16)
        width = pl.ds(pl.multiple_of(h * group * dim, dim), group * dim)
        pltpu.make_async_copy(qo.at[:, width], qo_hbm.at[:, width], out_sem.at[h]).start()
        return 0

    lax.fori_loop(0, kv_heads, query_side, 0)

    def norm_back(x, upstream):
        r = key_factor(x)
        w = upstream * both
        inner = jnp.mean(w * x, axis=-1, keepdims=True)
        return r * w - x * (r * r * r) * inner

    half = kv_heads * dim
    for h in range(kv_heads):
        drain(rs_dst.at[h], rs_recv.at[h])
        sums = jnp.sum(rs_dst[h].astype(F32), axis=0)
        at = slice(h * dim, (h + 1) * dim)
        x = pkv[me, 0, :, at].astype(F32)
        w = sums[:, :dim] * gk * gq
        r = key_factor(x)
        inner = jnp.mean(w * x, axis=-1, keepdims=True)
        ag[me, :, at] = (r * w - x * (r * r * r) * inner).astype(BF16)
        ag[me, :, half + h * dim : half + (h + 1) * dim] = sums[:, dim:].astype(BF16)
    send_all(remote(lambda peer: ag.at[me], ag.at[me], ag_send, ag_recv))

    for h in range(kv_heads):
        at = slice(h * dim, (h + 1) * dim)
        ko_ref[:, at] = norm_back(kv[:, at].astype(F32), acc[h, :, :dim]).astype(BF16)
        vo_ref[:, at] = acc[h, :, dim:].astype(BF16)

    drain(ag, ag_recv)
    grads = ag[...].astype(F32).reshape(prompt, 2 * half).astype(BF16)
    piece = dot_nt(grads, wv[...])
    hs_src[...] = piece.reshape(n, per, piece.shape[1]).astype(BF16)
    send_all(remote(lambda peer: hs_src.at[peer], hs_dst.at[me], hs_send, hs_recv))
    hs_dst[me] = hs_src[me]

    def finish(h, _):
        width = pl.ds(pl.multiple_of(h * group * dim, dim), group * dim)
        pltpu.make_async_copy(qo.at[:, width], qo_hbm.at[:, width], out_sem.at[h]).wait()
        drain(rs_src.at[h], rs_send.at[h])
        return 0

    lax.fori_loop(0, kv_heads, finish, 0)
    drain(pkv, pg_send)
    drain(ag, ag_send)
    drain(hs_src, hs_send)
    drain(hs_dst, hs_recv)
    ho_ref[...] = hs_dst[...]


def solution(mesh):
    n = mesh.shape["cand"]

    def on_device(pk, pv, q, k, v, g, lengths, seen, gq, gk, w):
        dim = gq.shape[0]
        slots, q_width = q.shape
        kv_heads = k.shape[1] // dim
        group = q_width // (kv_heads * dim)
        wide = 2 if group % 2 == 0 else 1
        per = pk.shape[0]
        m = w.shape[0]
        prompt = n * per
        total = prompt + slots
        smem = pl.BlockSpec(memory_space=pltpu.SMEM)
        vmem = pl.BlockSpec(memory_space=pltpu.VMEM)
        anywhere = pl.BlockSpec(memory_space=pl.ANY)
        qo, ko, vo, ho = pl.pallas_call(
            functools.partial(kernel, n),
            out_shape=(
                jax.ShapeDtypeStruct(q.shape, BF16),
                jax.ShapeDtypeStruct(k.shape, BF16),
                jax.ShapeDtypeStruct(v.shape, BF16),
                jax.ShapeDtypeStruct((n, per, m), BF16),
            ),
            in_specs=[smem, smem, vmem, vmem] + [anywhere] * 7,
            out_specs=(anywhere, vmem, vmem, vmem),
            scratch_shapes=[
                pltpu.VMEM((n, 2) + pk.shape, BF16),
                pltpu.VMEM(q.shape, BF16),
                pltpu.VMEM(k.shape, BF16),
                pltpu.VMEM(v.shape, BF16),
                pltpu.VMEM(g.shape, BF16),
                pltpu.VMEM(w.shape, BF16),
                pltpu.VMEM((total, wide * slots), F32),
                pltpu.VMEM((kv_heads, group // wide, total, wide * slots), BF16),
                pltpu.VMEM((kv_heads, group // wide, dim, wide * slots), F32),
                pltpu.VMEM((kv_heads, dim, total), BF16),
                pltpu.VMEM((kv_heads, slots, 2 * dim), F32),
                pltpu.VMEM(q.shape, BF16),
                pltpu.VMEM((kv_heads, n, per, 2 * dim), BF16),
                pltpu.VMEM((kv_heads, n, per, 2 * dim), BF16),
                pltpu.VMEM((n, per, 2 * kv_heads * dim), BF16),
                pltpu.VMEM((n, per, m), BF16),
                pltpu.VMEM((n, per, m), BF16),
                pltpu.SemaphoreType.DMA((2,)),
                pltpu.SemaphoreType.DMA((5,)),
                pltpu.SemaphoreType.DMA((kv_heads,)),
                pltpu.SemaphoreType.DMA,
                pltpu.SemaphoreType.DMA,
                pltpu.SemaphoreType.DMA((kv_heads,)),
                pltpu.SemaphoreType.DMA((kv_heads,)),
                pltpu.SemaphoreType.DMA,
                pltpu.SemaphoreType.DMA,
                pltpu.SemaphoreType.DMA,
                pltpu.SemaphoreType.DMA,
            ],
            compiler_params=pltpu.CompilerParams(
                collective_id=0,
                has_side_effects=True,
                vmem_limit_bytes=60 * 1024 * 1024,
            ),
        )(lengths, seen, gq, gk, pk, pv, q, k, v, g, w)
        hidden = jnp.transpose(ho, (1, 0, 2)).reshape(per, n * m)
        return qo, ko, vo, hidden

    rows = P(("grp", "cand"), None)
    return jax.shard_map(
        on_device,
        mesh=mesh,
        in_specs=(rows,) * 6 + (P(("grp", "cand")), P(("grp", "cand")), P(), P(), P("cand", None)),
        out_specs=(rows,) * 4,
        check_vma=False,
    )
```

```python
import functools
import math

import jax
import jax.numpy as jnp
from jax import lax
from jax.experimental import pallas as pl
from jax.experimental.pallas import tpu as pltpu
from jax.sharding import PartitionSpec as P

EPS = 1e-06
F32 = jnp.float32
BF16 = jnp.bfloat16


def dot_nt(a, b):
    return lax.dot_general(a, b, (((1,), (1,)), ((), ())), preferred_element_type=F32)


def dot_nn(a, b):
    return lax.dot_general(a, b, (((1,), (0,)), ((), ())), preferred_element_type=F32)


def kernel(
    n,
    len_ref,
    seen_ref,
    gq_hbm,
    gk_hbm,
    pk_hbm,
    pv_hbm,
    q_hbm,
    k_hbm,
    v_hbm,
    g_hbm,
    w_hbm,
    qo,
    ko_ref,
    vo_ref,
    ho_ref,
    gq_ref,
    gk_ref,
    pkv,
    qv,
    kv,
    vv,
    gv,
    wv,
    mask,
    dsv,
    xcv,
    kgt,
    acc,
    rs_src,
    rs_dst,
    ag,
    hs_src,
    hs_dst,
    own_sem,
    in_sem,
    pg_send,
    pg_recv,
    rs_send,
    rs_recv,
    ag_send,
    ag_recv,
    hs_send,
    hs_recv,
):
    me = lax.axis_index("cand")
    slots, q_width = qv.shape
    kv_heads = rs_src.shape[0]
    per = pkv.shape[3]
    dim = gq_ref.shape[0]
    prompt = n * per
    total = prompt + slots
    group = q_width // (kv_heads * dim)
    wide = 2 if group % 2 == 0 else 1
    pairs = group // wide
    lanes = wide * slots
    scale = dim ** (-0.5)

    own = [
        pltpu.make_async_copy(
            src.at[:, h * dim : (h + 1) * dim], pkv.at[h, me, i], own_sem.at[i, h]
        )
        for i, src in enumerate((pk_hbm, pv_hbm))
        for h in range(kv_heads)
    ]
    loads = [
        pltpu.make_async_copy(src, dst, in_sem.at[i])
        for i, (src, dst) in enumerate(
            (
                (gq_hbm, gq_ref),
                (gk_hbm, gk_ref),
                (k_hbm, kv),
                (v_hbm, vv),
                (q_hbm, qv),
                (g_hbm, gv),
                (w_hbm, wv),
            )
        )
    ]
    for copy in own:
        copy.start()

    barrier = pltpu.get_barrier_semaphore()

    def greet(step, _):
        peer = lax.rem(me + step, n)
        pl.semaphore_signal(
            barrier, inc=1, device_id={"cand": peer}, device_id_type=pl.DeviceIdType.MESH
        )
        return 0

    lax.fori_loop(1, n, greet, 0)
    for copy in loads[:-1]:
        copy.start()
    pl.semaphore_wait(barrier, n - 1)

    def send_all(copy_of):
        def body(step, _):
            copy_of(lax.rem(me + step, n)).start()
            return 0

        lax.fori_loop(1, n, body, 0)

    def remote(src, dst, send, recv):
        def copy_of(peer):
            return pltpu.make_async_remote_copy(
                src_ref=src(peer),
                dst_ref=dst,
                send_sem=send,
                recv_sem=recv,
                device_id={"cand": peer},
                device_id_type=pl.DeviceIdType.MESH,
            )

        return copy_of

    def drain(buffer, sem):
        part = buffer.at[pl.ds(0, n - 1)]
        pltpu.make_async_copy(part, part, sem).wait()

    for copy in own:
        copy.wait()
    for h in range(kv_heads):
        send_all(
            remote(
                lambda peer, h=h: pkv.at[h, me], pkv.at[h, me], pg_send.at[h], pg_recv.at[h]
            )
        )
    loads[-1].start()
    for copy in loads[:2]:
        copy.wait()

    gq = gq_ref[...].reshape(1, dim)
    gk = gk_ref[...].reshape(1, dim)
    both = gq * gk
    row = lax.broadcasted_iota(jnp.int32, (slots, dim), 0)
    live = (row < len_ref[0]).astype(F32).astype(BF16)
    key = lax.broadcasted_iota(jnp.int32, (prompt, slots), 0)
    seen = (key < seen_ref[0]).astype(F32)
    slot_j = lax.broadcasted_iota(jnp.int32, (slots, slots), 0)
    slot_i = lax.broadcasted_iota(jnp.int32, (slots, slots), 1)
    causal = (slot_j <= slot_i).astype(F32)
    for b in range(wide):
        mask[:prompt, b * slots : (b + 1) * slots] = seen
        mask[prompt:, b * slots : (b + 1) * slots] = causal
    eye_r = lax.broadcasted_iota(jnp.int32, (dim, dim), 0)
    eye_c = lax.broadcasted_iota(jnp.int32, (dim, dim), 1)
    eye = (eye_r == eye_c).astype(F32).astype(BF16)

    def head_lanes(head):
        return pl.ds(pl.multiple_of(head * dim, dim), dim)

    def key_factor(x):
        return lax.rsqrt(jnp.mean(x * x, axis=-1, keepdims=True) + EPS)

    for copy in loads[2:-1]:
        copy.wait()

    def forward(h, _):
        drain(pkv.at[h], pg_recv.at[h])
        raw = jnp.concatenate(
            [
                pkv[h, :, 0].astype(F32).reshape(prompt, dim),
                kv[:, head_lanes(h)].astype(F32),
            ],
            axis=0,
        )
        kg32 = raw * key_factor(raw) * both
        kgt[h] = kg32.T.astype(BF16)
        left = jnp.concatenate([kg32.astype(BF16), eye], axis=0)
        val = jnp.concatenate(
            [
                pkv[h, :, 1].astype(F32).reshape(prompt, dim).astype(BF16),
                vv[:, head_lanes(h)],
            ],
            axis=0,
        )
        dk = dv = None
        for b in range(pairs):
            heads = [h * group + b * wide + a for a in range(wide)]
            x2 = jnp.concatenate([qv[:, head_lanes(a)] for a in heads], axis=0)
            g2 = jnp.concatenate([gv[:, head_lanes(a)] * live for a in heads], axis=0)
            both_t = dot_nt(left, x2)
            x_t = both_t[total:]
            r = lax.rsqrt(jnp.mean(x_t * x_t, axis=0, keepdims=True) + EPS)
            z = both_t[:total] * (r * (scale * math.log2(math.e)))
            e = jnp.exp2(z) * mask[...]
            dp = dot_nt(val, g2)
            inv = 1.0 / jnp.sum(e, axis=0, keepdims=True)
            p = e * inv
            delta = jnp.sum(p * dp, axis=0, keepdims=True)
            ds = p * (dp - delta)
            inner = jnp.sum(ds * z, axis=0, keepdims=True)
            xcv[h, b] = x_t * (r * r * inner * (math.log(2.0) / dim))
            ds = (ds * (r * scale)).astype(BF16)
            dsv[h, b] = ds
            dv_b = dot_nn(p.astype(BF16), g2)
            dk_b = dot_nn(ds, x2)
            dv = dv_b if dv is None else dv + dv_b
            dk = dk_b if dk is None else dk + dk_b
        rs_src[h, :, :, :dim] = dk[:prompt].reshape(n, per, dim).astype(BF16)
        rs_src[h, :, :, dim:] = dv[:prompt].reshape(n, per, dim).astype(BF16)
        send_all(
            remote(
                lambda peer: rs_src.at[h, peer],
                rs_dst.at[h, me],
                rs_send.at[h],
                rs_recv.at[h],
            )
        )
        rs_dst[h, me] = rs_src[h, me]
        acc[h, :, :dim] = dk[prompt:]
        acc[h, :, dim:] = dv[prompt:]
        return 0

    lax.fori_loop(0, kv_heads, forward, 0)

    def query_side(h, _):
        for b in range(pairs):
            dx = dot_nn(kgt[h], dsv[h, b]) - xcv[h, b]
            for a in range(wide):
                head = h * group + b * wide + a
                qo[:, head_lanes(head)] = dx[:, a * slots : (a + 1) * slots].T.astype(BF16)
        return 0

    lax.fori_loop(0, kv_heads, query_side, 0)

    def norm_back(x, upstream):
        r = key_factor(x)
        w = upstream * both
        inner = jnp.mean(w * x, axis=-1, keepdims=True)
        return r * w - x * (r * r * r) * inner

    for h in range(kv_heads):
        at = slice(h * dim, (h + 1) * dim)
        ko_ref[:, at] = norm_back(kv[:, at].astype(F32), acc[h, :, :dim]).astype(BF16)
        vo_ref[:, at] = acc[h, :, dim:].astype(BF16)

    for h in range(kv_heads):
        drain(rs_dst.at[h], rs_recv.at[h])
        sums = jnp.sum(rs_dst[h].astype(F32), axis=0)
        dk = norm_back(pkv[h, me, 0].astype(F32), sums[:, :dim])
        ag[h, me] = jnp.concatenate([dk, sums[:, dim:]], axis=1).astype(BF16)
        send_all(
            remote(
                lambda peer, h=h: ag.at[h, me], ag.at[h, me], ag_send.at[h], ag_recv.at[h]
            )
        )

    loads[-1].wait()
    half = kv_heads * dim
    piece = None
    for h in range(kv_heads):
        drain(ag.at[h], ag_recv.at[h])
        grads = ag[h].astype(F32).reshape(prompt, 2 * dim).astype(BF16)
        at = slice(h * dim, (h + 1) * dim)
        w_h = jnp.concatenate(
            [wv[:, at], wv[:, half + h * dim : half + (h + 1) * dim]], axis=1
        )
        part = dot_nt(grads, w_h)
        piece = part if piece is None else piece + part
    hs_src[...] = piece.reshape(n, per, piece.shape[1]).astype(BF16)
    send_all(remote(lambda peer: hs_src.at[peer], hs_dst.at[me], hs_send, hs_recv))
    hs_dst[me] = hs_src[me]

    def finish(h, _):
        drain(rs_src.at[h], rs_send.at[h])
        drain(pkv.at[h], pg_send.at[h])
        drain(ag.at[h], ag_send.at[h])
        return 0

    lax.fori_loop(0, kv_heads, finish, 0)
    drain(hs_src, hs_send)
    drain(hs_dst, hs_recv)
    ho_ref[...] = hs_dst[...]


def write_out(qo, ko, vo, ho, q_hbm, k_hbm, v_hbm, h_hbm, hidden, sem):
    copies = [
        pltpu.make_async_copy(src, dst, sem.at[i])
        for i, (src, dst) in enumerate(((qo, q_hbm), (ko, k_hbm), (vo, v_hbm), (hidden, h_hbm)))
    ]
    for copy in copies[:3]:
        copy.start()
    hidden[...] = jnp.concatenate(
        [ho[i].astype(F32) for i in range(ho.shape[0])], axis=1
    ).astype(BF16)
    copies[3].start()
    for copy in copies:
        copy.wait()


def solution(mesh):
    n = mesh.shape["cand"]

    def on_device(pk, pv, q, k, v, g, lengths, seen, gq, gk, w):
        dim = gq.shape[0]
        slots, q_width = q.shape
        kv_heads = k.shape[1] // dim
        group = q_width // (kv_heads * dim)
        wide = 2 if group % 2 == 0 else 1
        per = pk.shape[0]
        m = w.shape[0]
        prompt = n * per
        total = prompt + slots
        smem = pl.BlockSpec(memory_space=pltpu.SMEM)
        vmem = pl.BlockSpec(memory_space=pltpu.VMEM)
        anywhere = pl.BlockSpec(memory_space=pl.ANY)
        qo, ko, vo, ho = pl.pallas_call(
            functools.partial(kernel, n),
            out_shape=(
                pltpu.VMEM(q.shape, BF16),
                pltpu.VMEM(k.shape, BF16),
                pltpu.VMEM(v.shape, BF16),
                pltpu.VMEM((n, per, m), BF16),
            ),
            in_specs=[smem] * 2 + [pl.BlockSpec(memory_space=pltpu.HBM)] * 9,
            out_specs=(vmem,) * 4,
            scratch_shapes=[
                pltpu.VMEM(gq.shape, F32),
                pltpu.VMEM(gk.shape, F32),
                pltpu.VMEM((kv_heads, n, 2, per, dim), BF16),
                pltpu.VMEM(q.shape, BF16),
                pltpu.VMEM(k.shape, BF16),
                pltpu.VMEM(v.shape, BF16),
                pltpu.VMEM(g.shape, BF16),
                pltpu.VMEM(w.shape, BF16),
                pltpu.VMEM((total, wide * slots), F32),
                pltpu.VMEM((kv_heads, group // wide, total, wide * slots), BF16),
                pltpu.VMEM((kv_heads, group // wide, dim, wide * slots), F32),
                pltpu.VMEM((kv_heads, dim, total), BF16),
                pltpu.VMEM((kv_heads, slots, 2 * dim), F32),
                pltpu.VMEM((kv_heads, n, per, 2 * dim), BF16),
                pltpu.VMEM((kv_heads, n, per, 2 * dim), BF16),
                pltpu.VMEM((kv_heads, n, per, 2 * dim), BF16),
                pltpu.VMEM((n, per, m), BF16),
                pltpu.VMEM((n, per, m), BF16),
                pltpu.SemaphoreType.DMA((2, kv_heads)),
                pltpu.SemaphoreType.DMA((7,)),
            ]
            + [pltpu.SemaphoreType.DMA((kv_heads,))] * 6
            + [pltpu.SemaphoreType.DMA] * 2,
            compiler_params=pltpu.CompilerParams(
                collective_id=0,
                has_side_effects=True,
                vmem_limit_bytes=48 * 1024 * 1024,
            ),
        )(
            lengths,
            seen,
            *[
                pltpu.with_memory_space_constraint(x, pltpu.HBM)
                for x in (gq, gk, pk, pv, q, k, v, g, w)
            ],
        )
        return pl.pallas_call(
            write_out,
            out_shape=(
                jax.ShapeDtypeStruct(q.shape, BF16),
                jax.ShapeDtypeStruct(k.shape, BF16),
                jax.ShapeDtypeStruct(v.shape, BF16),
                jax.ShapeDtypeStruct((per, n * m), BF16),
            ),
            in_specs=[vmem] * 4,
            out_specs=(anywhere,) * 4,
            scratch_shapes=[
                pltpu.VMEM((per, n * m), BF16),
                pltpu.SemaphoreType.DMA((4,)),
            ],
            compiler_params=pltpu.CompilerParams(vmem_limit_bytes=8 * 1024 * 1024),
        )(*[pltpu.with_memory_space_constraint(x, pltpu.VMEM) for x in (qo, ko, vo, ho)])

    rows = P(("grp", "cand"), None)
    return jax.shard_map(
        on_device,
        mesh=mesh,
        in_specs=(rows,) * 6 + (P(("grp", "cand")), P(("grp", "cand")), P(), P(), P("cand", None)),
        out_specs=(rows,) * 4,
        check_vma=False,
    )
```

```python
import functools
import math

import jax
import jax.numpy as jnp
from jax import lax
from jax.experimental import pallas as pl
from jax.experimental.pallas import tpu as pltpu
from jax.sharding import PartitionSpec as P

EPS = 1e-06
F32 = jnp.float32
BF16 = jnp.bfloat16


def dot_nt(a, b):
    return lax.dot_general(a, b, (((1,), (1,)), ((), ())), preferred_element_type=F32)


def dot_nn(a, b):
    return lax.dot_general(a, b, (((1,), (0,)), ((), ())), preferred_element_type=F32)


def kernel(
    n,
    len_ref,
    seen_ref,
    gq_hbm,
    gk_hbm,
    pk_hbm,
    pv_hbm,
    q_hbm,
    k_hbm,
    v_hbm,
    g_hbm,
    w_hbm,
    qo,
    ko_ref,
    vo_ref,
    ho_ref,
    gq_ref,
    gk_ref,
    pkv,
    qv,
    kv,
    vv,
    gv,
    wv,
    mask,
    ev,
    dpv,
    pv,
    dsv,
    xcv,
    kgt,
    acc,
    rs_src,
    rs_dst,
    ag,
    hs_src,
    hs_dst,
    own_sem,
    in_sem,
    pg_send,
    pg_recv,
    rs_send,
    rs_recv,
    ag_send,
    ag_recv,
    hs_send,
    hs_recv,
):
    me = lax.axis_index("cand")
    slots, q_width = qv.shape
    kv_heads = rs_src.shape[0]
    per = pkv.shape[3]
    dim = gq_ref.shape[0]
    prompt = n * per
    total = prompt + slots
    group = q_width // (kv_heads * dim)
    wide = 2 if group % 2 == 0 else 1
    pairs = group // wide
    lanes = wide * slots
    chunk = math.gcd(total, 64)
    scale = dim ** (-0.5)

    own = [
        pltpu.make_async_copy(
            src.at[:, h * dim : (h + 1) * dim], pkv.at[h, me, i], own_sem.at[i, h]
        )
        for i, src in enumerate((pk_hbm, pv_hbm))
        for h in range(kv_heads)
    ]
    loads = [
        pltpu.make_async_copy(src, dst, in_sem.at[i])
        for i, (src, dst) in enumerate(
            (
                (gq_hbm, gq_ref),
                (gk_hbm, gk_ref),
                (k_hbm, kv),
                (v_hbm, vv),
                (q_hbm, qv),
                (g_hbm, gv),
                (w_hbm, wv),
            )
        )
    ]
    for copy in own:
        copy.start()

    barrier = pltpu.get_barrier_semaphore()

    def greet(step, _):
        peer = lax.rem(me + step, n)
        pl.semaphore_signal(
            barrier, inc=1, device_id={"cand": peer}, device_id_type=pl.DeviceIdType.MESH
        )
        return 0

    lax.fori_loop(1, n, greet, 0)
    for copy in loads[:-1]:
        copy.start()
    pl.semaphore_wait(barrier, n - 1)

    def send_all(copy_of):
        def body(step, _):
            copy_of(lax.rem(me + step, n)).start()
            return 0

        lax.fori_loop(1, n, body, 0)

    def remote(src, dst, send, recv):
        def copy_of(peer):
            return pltpu.make_async_remote_copy(
                src_ref=src(peer),
                dst_ref=dst,
                send_sem=send,
                recv_sem=recv,
                device_id={"cand": peer},
                device_id_type=pl.DeviceIdType.MESH,
            )

        return copy_of

    def drain(buffer, sem):
        part = buffer.at[pl.ds(0, n - 1)]
        pltpu.make_async_copy(part, part, sem).wait()

    for copy in own:
        copy.wait()
    for h in range(kv_heads):
        send_all(
            remote(
                lambda peer, h=h: pkv.at[h, me], pkv.at[h, me], pg_send.at[h], pg_recv.at[h]
            )
        )
    loads[-1].start()
    for copy in loads[:2]:
        copy.wait()

    gq = gq_ref[...].reshape(1, dim)
    gk = gk_ref[...].reshape(1, dim)
    both = gq * gk
    row = lax.broadcasted_iota(jnp.int32, (slots, dim), 0)
    live = (row < len_ref[0]).astype(F32).astype(BF16)
    key = lax.broadcasted_iota(jnp.int32, (prompt, slots), 0)
    seen = (key < seen_ref[0]).astype(F32)
    slot_j = lax.broadcasted_iota(jnp.int32, (slots, slots), 0)
    slot_i = lax.broadcasted_iota(jnp.int32, (slots, slots), 1)
    causal = (slot_j <= slot_i).astype(F32)
    for b in range(wide):
        mask[:prompt, b * slots : (b + 1) * slots] = seen
        mask[prompt:, b * slots : (b + 1) * slots] = causal
    eye_r = lax.broadcasted_iota(jnp.int32, (dim, dim), 0)
    eye_c = lax.broadcasted_iota(jnp.int32, (dim, dim), 1)
    eye = (eye_r == eye_c).astype(F32).astype(BF16)

    def head_lanes(head):
        return pl.ds(pl.multiple_of(head * dim, dim), dim)

    def key_factor(x):
        return lax.rsqrt(jnp.mean(x * x, axis=-1, keepdims=True) + EPS)

    for copy in loads[2:-1]:
        copy.wait()

    def forward(h, _):
        drain(pkv.at[h], pg_recv.at[h])
        raw = jnp.concatenate(
            [
                pkv[h, :, 0].astype(F32).reshape(prompt, dim),
                kv[:, head_lanes(h)].astype(F32),
            ],
            axis=0,
        )
        kg32 = raw * key_factor(raw) * both
        kgt[h] = kg32.T.astype(BF16)
        left = jnp.concatenate([kg32.astype(BF16), eye], axis=0)
        val = jnp.concatenate(
            [
                pkv[h, :, 1].astype(F32).reshape(prompt, dim).astype(BF16),
                vv[:, head_lanes(h)],
            ],
            axis=0,
        )
        heads = [qv[:, head_lanes(h * group + a)] for a in range(group)]
        x_all = jnp.concatenate(heads, axis=0)
        heads = [gv[:, head_lanes(h * group + a)] * live for a in range(group)]
        g_all = jnp.concatenate(heads, axis=0)
        for b in range(pairs):
            at = slice(b * lanes, (b + 1) * lanes)
            both_t = dot_nt(left, x_all[at])
            ev[b] = both_t[:total]
            x_t = both_t[total:]
            r = lax.rsqrt(jnp.mean(x_t * x_t, axis=0, keepdims=True) + EPS)
            xcv[h, :, at] = x_t * r
            dpv[b] = dot_nt(val, g_all[at])
            up = r * (scale * math.log2(math.e))
            tops = inner = jnp.zeros((8, lanes), F32)
            for c in range(0, total, chunk):
                rows = slice(c, c + chunk)
                e = jnp.exp2(ev[b, rows] * up) * mask[rows]
                ev[b, rows] = e
                tops = tops + jnp.sum(e.reshape(chunk // 8, 8, lanes), axis=0)
                inner = inner + jnp.sum(
                    (e * dpv[b, rows]).reshape(chunk // 8, 8, lanes), axis=0
                )
            inv = 1.0 / jnp.sum(tops, axis=0, keepdims=True)
            delta = jnp.sum(inner, axis=0, keepdims=True) * inv
            down = inv * (r * scale)
            for c in range(0, total, chunk):
                rows = slice(c, c + chunk)
                e = ev[b, rows]
                pv[rows, at] = (e * inv).astype(BF16)
                dsv[h, rows, at] = (e * (dpv[b, rows] - delta) * down).astype(BF16)
        dv = dot_nn(pv[...], g_all)
        dk = dot_nn(dsv[h], x_all)
        rs_src[h, :, :, :dim] = dk[:prompt].reshape(n, per, dim).astype(BF16)
        rs_src[h, :, :, dim:] = dv[:prompt].reshape(n, per, dim).astype(BF16)
        send_all(
            remote(
                lambda peer: rs_src.at[h, peer],
                rs_dst.at[h, me],
                rs_send.at[h],
                rs_recv.at[h],
            )
        )
        rs_dst[h, me] = rs_src[h, me]
        acc[h, :, :dim] = dk[prompt:]
        acc[h, :, dim:] = dv[prompt:]
        return 0

    lax.fori_loop(0, kv_heads, forward, 0)

    def query_side(h, _):
        for b in range(pairs):
            at = slice(b * lanes, (b + 1) * lanes)
            dq = dot_nn(kgt[h], dsv[h, :, at])
            x_t = xcv[h, :, at]
            dx = dq - x_t * jnp.mean(dq * x_t, axis=0, keepdims=True)
            for a in range(wide):
                head = h * group + b * wide + a
                qo[:, head_lanes(head)] = dx[:, a * slots : (a + 1) * slots].T.astype(BF16)
        return 0

    lax.fori_loop(0, kv_heads, query_side, 0)

    def norm_back(x, upstream):
        r = key_factor(x)
        w = upstream * both
        inner = jnp.mean(w * x, axis=-1, keepdims=True)
        return r * w - x * (r * r * r) * inner

    for h in range(kv_heads):
        at = slice(h * dim, (h + 1) * dim)
        ko_ref[:, at] = norm_back(kv[:, at].astype(F32), acc[h, :, :dim]).astype(BF16)
        vo_ref[:, at] = acc[h, :, dim:].astype(BF16)

    for h in range(kv_heads):
        drain(rs_dst.at[h], rs_recv.at[h])
        sums = jnp.sum(rs_dst[h].astype(F32), axis=0)
        dk = norm_back(pkv[h, me, 0].astype(F32), sums[:, :dim])
        ag[h, me] = jnp.concatenate([dk, sums[:, dim:]], axis=1).astype(BF16)
        send_all(
            remote(
                lambda peer, h=h: ag.at[h, me], ag.at[h, me], ag_send.at[h], ag_recv.at[h]
            )
        )

    loads[-1].wait()
    half = kv_heads * dim
    piece = None
    for h in range(kv_heads):
        drain(ag.at[h], ag_recv.at[h])
        grads = ag[h].astype(F32).reshape(prompt, 2 * dim).astype(BF16)
        at = slice(h * dim, (h + 1) * dim)
        w_h = jnp.concatenate(
            [wv[:, at], wv[:, half + h * dim : half + (h + 1) * dim]], axis=1
        )
        part = dot_nt(grads, w_h)
        piece = part if piece is None else piece + part
    hs_src[...] = piece.reshape(n, per, piece.shape[1]).astype(BF16)
    send_all(remote(lambda peer: hs_src.at[peer], hs_dst.at[me], hs_send, hs_recv))
    hs_dst[me] = hs_src[me]

    def finish(h, _):
        drain(rs_src.at[h], rs_send.at[h])
        drain(pkv.at[h], pg_send.at[h])
        drain(ag.at[h], ag_send.at[h])
        return 0

    lax.fori_loop(0, kv_heads, finish, 0)
    drain(hs_src, hs_send)
    drain(hs_dst, hs_recv)
    ho_ref[...] = hs_dst[...]


def write_out(qo, ko, vo, ho, q_hbm, k_hbm, v_hbm, h_hbm, hidden, sem):
    copies = [
        pltpu.make_async_copy(src, dst, sem.at[i])
        for i, (src, dst) in enumerate(((qo, q_hbm), (ko, k_hbm), (vo, v_hbm), (hidden, h_hbm)))
    ]
    for copy in copies[:3]:
        copy.start()
    hidden[...] = jnp.concatenate(
        [ho[i].astype(F32) for i in range(ho.shape[0])], axis=1
    ).astype(BF16)
    copies[3].start()
    for copy in copies:
        copy.wait()


def solution(mesh):
    n = mesh.shape["cand"]

    def on_device(pk, pv, q, k, v, g, lengths, seen, gq, gk, w):
        dim = gq.shape[0]
        slots, q_width = q.shape
        kv_heads = k.shape[1] // dim
        group = q_width // (kv_heads * dim)
        wide = 2 if group % 2 == 0 else 1
        per = pk.shape[0]
        m = w.shape[0]
        prompt = n * per
        total = prompt + slots
        smem = pl.BlockSpec(memory_space=pltpu.SMEM)
        vmem = pl.BlockSpec(memory_space=pltpu.VMEM)
        anywhere = pl.BlockSpec(memory_space=pl.ANY)
        qo, ko, vo, ho = pl.pallas_call(
            functools.partial(kernel, n),
            out_shape=(
                pltpu.VMEM(q.shape, BF16),
                pltpu.VMEM(k.shape, BF16),
                pltpu.VMEM(v.shape, BF16),
                pltpu.VMEM((n, per, m), BF16),
            ),
            in_specs=[smem] * 2 + [pl.BlockSpec(memory_space=pltpu.HBM)] * 9,
            out_specs=(vmem,) * 4,
            scratch_shapes=[
                pltpu.VMEM(gq.shape, F32),
                pltpu.VMEM(gk.shape, F32),
                pltpu.VMEM((kv_heads, n, 2, per, dim), BF16),
                pltpu.VMEM(q.shape, BF16),
                pltpu.VMEM(k.shape, BF16),
                pltpu.VMEM(v.shape, BF16),
                pltpu.VMEM(g.shape, BF16),
                pltpu.VMEM(w.shape, BF16),
                pltpu.VMEM((total, wide * slots), F32),
                pltpu.VMEM((group // wide, total, wide * slots), F32),
                pltpu.VMEM((group // wide, total, wide * slots), F32),
                pltpu.VMEM((total, group * slots), BF16),
                pltpu.VMEM((kv_heads, total, group * slots), BF16),
                pltpu.VMEM((kv_heads, dim, group * slots), F32),
                pltpu.VMEM((kv_heads, dim, total), BF16),
                pltpu.VMEM((kv_heads, slots, 2 * dim), F32),
                pltpu.VMEM((kv_heads, n, per, 2 * dim), BF16),
                pltpu.VMEM((kv_heads, n, per, 2 * dim), BF16),
                pltpu.VMEM((kv_heads, n, per, 2 * dim), BF16),
                pltpu.VMEM((n, per, m), BF16),
                pltpu.VMEM((n, per, m), BF16),
                pltpu.SemaphoreType.DMA((2, kv_heads)),
                pltpu.SemaphoreType.DMA((7,)),
            ]
            + [pltpu.SemaphoreType.DMA((kv_heads,))] * 6
            + [pltpu.SemaphoreType.DMA] * 2,
            compiler_params=pltpu.CompilerParams(
                collective_id=0,
                has_side_effects=True,
                vmem_limit_bytes=48 * 1024 * 1024,
            ),
        )(
            lengths,
            seen,
            *[
                pltpu.with_memory_space_constraint(x, pltpu.HBM)
                for x in (gq, gk, pk, pv, q, k, v, g, w)
            ],
        )
        return pl.pallas_call(
            write_out,
            out_shape=(
                jax.ShapeDtypeStruct(q.shape, BF16),
                jax.ShapeDtypeStruct(k.shape, BF16),
                jax.ShapeDtypeStruct(v.shape, BF16),
                jax.ShapeDtypeStruct((per, n * m), BF16),
            ),
            in_specs=[vmem] * 4,
            out_specs=(anywhere,) * 4,
            scratch_shapes=[
                pltpu.VMEM((per, n * m), BF16),
                pltpu.SemaphoreType.DMA((4,)),
            ],
            compiler_params=pltpu.CompilerParams(vmem_limit_bytes=8 * 1024 * 1024),
        )(*[pltpu.with_memory_space_constraint(x, pltpu.VMEM) for x in (qo, ko, vo, ho)])

    rows = P(("grp", "cand"), None)
    return jax.shard_map(
        on_device,
        mesh=mesh,
        in_specs=(rows,) * 6 + (P(("grp", "cand")), P(("grp", "cand")), P(), P(), P("cand", None)),
        out_specs=(rows,) * 4,
        check_vma=False,
    )
```

```python
import functools
import math

import jax
import jax.numpy as jnp
from jax import lax
from jax.experimental import pallas as pl
from jax.experimental.pallas import tpu as pltpu
from jax.sharding import PartitionSpec as P

EPS = 1e-06
F32 = jnp.float32
BF16 = jnp.bfloat16


def dot_nt(a, b):
    return lax.dot_general(a, b, (((1,), (1,)), ((), ())), preferred_element_type=F32)


def dot_nn(a, b):
    return lax.dot_general(a, b, (((1,), (0,)), ((), ())), preferred_element_type=F32)


def kernel(
    n,
    len_ref,
    seen_ref,
    gq_hbm,
    gk_hbm,
    pk_hbm,
    pv_hbm,
    q_hbm,
    k_hbm,
    v_hbm,
    g_hbm,
    w_hbm,
    qo,
    ko_ref,
    vo_ref,
    ho_ref,
    gq_ref,
    gk_ref,
    pkv,
    qv,
    kv,
    vv,
    gv,
    wv,
    mask,
    ev,
    dpv,
    er,
    dpr,
    pv,
    rv,
    sums_v,
    dsv,
    xcv,
    kgt,
    acc,
    rs_src,
    rs_dst,
    ag,
    hs_src,
    hs_dst,
    own_sem,
    in_sem,
    pg_send,
    pg_recv,
    rs_send,
    rs_recv,
    ag_send,
    ag_recv,
    hs_send,
    hs_recv,
):
    me = lax.axis_index("cand")
    slots, q_width = qv.shape
    kv_heads = rs_src.shape[0]
    per = pkv.shape[3]
    dim = gq_ref.shape[0]
    prompt = n * per
    total = prompt + slots
    group = q_width // (kv_heads * dim)
    wide = 2 if group % 2 == 0 else 1
    pairs = group // wide
    lanes = wide * slots
    chunk = math.gcd(math.gcd(prompt, slots), 64)
    scale = dim ** (-0.5)

    own = [
        pltpu.make_async_copy(
            src.at[:, h * dim : (h + 1) * dim], pkv.at[h, me, i], own_sem.at[i, h]
        )
        for i, src in enumerate((pk_hbm, pv_hbm))
        for h in range(kv_heads)
    ]
    loads = [
        pltpu.make_async_copy(src, dst, in_sem.at[i])
        for i, (src, dst) in enumerate(
            (
                (gq_hbm, gq_ref),
                (gk_hbm, gk_ref),
                (k_hbm, kv),
                (v_hbm, vv),
                (q_hbm, qv),
                (g_hbm, gv),
                (w_hbm, wv),
            )
        )
    ]
    for copy in own:
        copy.start()

    barrier = pltpu.get_barrier_semaphore()

    def greet(step, _):
        peer = lax.rem(me + step, n)
        pl.semaphore_signal(
            barrier, inc=1, device_id={"cand": peer}, device_id_type=pl.DeviceIdType.MESH
        )
        return 0

    lax.fori_loop(1, n, greet, 0, unroll=n <= 16)
    for copy in loads[:-1]:
        copy.start()
    pl.semaphore_wait(barrier, n - 1)

    def send_all(copy_of):
        def body(step, _):
            copy_of(lax.rem(me + step, n)).start()
            return 0

        lax.fori_loop(1, n, body, 0, unroll=n <= 16)

    def remote(src, dst, send, recv):
        def copy_of(peer):
            return pltpu.make_async_remote_copy(
                src_ref=src(peer),
                dst_ref=dst,
                send_sem=send,
                recv_sem=recv,
                device_id={"cand": peer},
                device_id_type=pl.DeviceIdType.MESH,
            )

        return copy_of

    def drain(buffer, sem):
        part = buffer.at[pl.ds(0, n - 1)]
        pltpu.make_async_copy(part, part, sem).wait()

    for copy in own:
        copy.wait()
    for h in range(kv_heads):
        send_all(
            remote(
                lambda peer, h=h: pkv.at[h, me], pkv.at[h, me], pg_send.at[h], pg_recv.at[h]
            )
        )
    loads[-1].start()
    for copy in loads[:2]:
        copy.wait()

    gq = gq_ref[...].reshape(1, dim)
    gk = gk_ref[...].reshape(1, dim)
    both = gq * gk
    row = lax.broadcasted_iota(jnp.int32, (slots, dim), 0)
    live = (row < len_ref[0]).astype(F32).astype(BF16)
    key = lax.broadcasted_iota(jnp.int32, (prompt, slots), 0)
    seen = (key < seen_ref[0]).astype(F32)
    slot_j = lax.broadcasted_iota(jnp.int32, (slots, slots), 0)
    slot_i = lax.broadcasted_iota(jnp.int32, (slots, slots), 1)
    causal = (slot_j <= slot_i).astype(F32)
    for b in range(wide):
        mask[:prompt, b * slots : (b + 1) * slots] = seen
        mask[prompt:, b * slots : (b + 1) * slots] = causal
    eye_r = lax.broadcasted_iota(jnp.int32, (dim, dim), 0)
    eye_c = lax.broadcasted_iota(jnp.int32, (dim, dim), 1)
    eye = (eye_r == eye_c).astype(F32).astype(BF16)

    def head_lanes(head):
        return pl.ds(pl.multiple_of(head * dim, dim), dim)

    def key_factor(x):
        return lax.rsqrt(jnp.mean(x * x, axis=-1, keepdims=True) + EPS)

    for copy in loads[2:-1]:
        copy.wait()

    def load_heads(h):
        heads = [qv[:, head_lanes(h * group + a)] for a in range(group)]
        x_all = jnp.concatenate(heads, axis=0)
        heads = [gv[:, head_lanes(h * group + a)] * live for a in range(group)]
        return x_all, jnp.concatenate(heads, axis=0)

    def lift(h, at, e_ref, dp_ref, first, tops, inner):
        up = rv[h, :, at] * (scale * math.log2(math.e))
        for c in range(0, e_ref.shape[0], chunk):
            rows = slice(c, c + chunk)
            e = jnp.exp2(e_ref[rows] * up) * mask[first + c : first + c + chunk]
            e_ref[rows] = e
            tops = tops + jnp.sum(e.reshape(chunk // 8, 8, lanes), axis=0)
            inner = inner + jnp.sum(
                (e * dp_ref[rows]).reshape(chunk // 8, 8, lanes), axis=0
            )
        return tops, inner

    def respond(h, _):
        raw = kv[:, head_lanes(h)].astype(F32)
        kg32 = raw * key_factor(raw) * both
        kgt[h, :, prompt:] = kg32.T.astype(BF16)
        left = jnp.concatenate([kg32.astype(BF16), eye], axis=0)
        val = vv[:, head_lanes(h)]
        x_all, g_all = load_heads(h)
        for b in range(pairs):
            at = slice(b * lanes, (b + 1) * lanes)
            both_t = dot_nt(left, x_all[at])
            er[h, b] = both_t[:slots]
            x_t = both_t[slots:]
            r = lax.rsqrt(jnp.mean(x_t * x_t, axis=0, keepdims=True) + EPS)
            rv[h, :, at] = r
            xcv[h, :, at] = x_t * r
            dpr[h, b] = dot_nt(val, g_all[at])
            zero = jnp.zeros((8, lanes), F32)
            tops, inner = lift(h, at, er.at[h, b], dpr.at[h, b], prompt, zero, zero)
            sums_v[h, 0, :, at] = tops
            sums_v[h, 1, :, at] = inner
        return 0

    lax.fori_loop(0, kv_heads, respond, 0)

    def forward(h, _):
        drain(pkv.at[h], pg_recv.at[h])
        raw = pkv[h, :, 0].astype(F32).reshape(prompt, dim)
        kg32 = raw * key_factor(raw) * both
        kgt[h, :, :prompt] = kg32.T.astype(BF16)
        left = kg32.astype(BF16)
        val = pkv[h, :, 1].astype(F32).reshape(prompt, dim).astype(BF16)
        x_all, g_all = load_heads(h)
        for b in range(pairs):
            at = slice(b * lanes, (b + 1) * lanes)
            ev[b] = dot_nt(left, x_all[at])
            dpv[b] = dot_nt(val, g_all[at])
            tops, inner = lift(
                h, at, ev.at[b], dpv.at[b], 0, sums_v[h, 0, :, at], sums_v[h, 1, :, at]
            )
            inv = 1.0 / jnp.sum(tops, axis=0, keepdims=True)
            delta = jnp.sum(inner, axis=0, keepdims=True) * inv
            down = inv * (rv[h, :, at] * scale)
            for first, e_ref, dp_ref in (
                (0, ev.at[b], dpv.at[b]),
                (prompt, er.at[h, b], dpr.at[h, b]),
            ):
                for c in range(0, e_ref.shape[0], chunk):
                    rows = slice(c, c + chunk)
                    to = slice(first + c, first + c + chunk)
                    e = e_ref[rows]
                    pv[to, at] = (e * inv).astype(BF16)
                    dsv[h, to, at] = (e * (dp_ref[rows] - delta) * down).astype(BF16)
        dv = dot_nn(pv[...], g_all)
        dk = dot_nn(dsv[h], x_all)
        rs_src[h, :, :, :dim] = dk[:prompt].reshape(n, per, dim).astype(BF16)
        rs_src[h, :, :, dim:] = dv[:prompt].reshape(n, per, dim).astype(BF16)
        send_all(
            remote(
                lambda peer: rs_src.at[h, peer],
                rs_dst.at[h, me],
                rs_send.at[h],
                rs_recv.at[h],
            )
        )
        rs_dst[h, me] = rs_src[h, me]
        acc[h, :, :dim] = dk[prompt:]
        acc[h, :, dim:] = dv[prompt:]
        return 0

    lax.fori_loop(0, kv_heads, forward, 0)

    def query_side(h, _):
        for b in range(pairs):
            at = slice(b * lanes, (b + 1) * lanes)
            dq = dot_nn(kgt[h], dsv[h, :, at])
            x_t = xcv[h, :, at]
            dx = dq - x_t * jnp.mean(dq * x_t, axis=0, keepdims=True)
            for a in range(wide):
                head = h * group + b * wide + a
                qo[:, head_lanes(head)] = dx[:, a * slots : (a + 1) * slots].T.astype(BF16)
        return 0

    lax.fori_loop(0, kv_heads, query_side, 0)

    def norm_back(x, upstream):
        r = key_factor(x)
        w = upstream * both
        inner = jnp.mean(w * x, axis=-1, keepdims=True)
        return r * w - x * (r * r * r) * inner

    for h in range(kv_heads):
        at = slice(h * dim, (h + 1) * dim)
        ko_ref[:, at] = norm_back(kv[:, at].astype(F32), acc[h, :, :dim]).astype(BF16)
        vo_ref[:, at] = acc[h, :, dim:].astype(BF16)

    for h in range(kv_heads):
        drain(rs_dst.at[h], rs_recv.at[h])
        sums = jnp.sum(rs_dst[h].astype(F32), axis=0)
        dk = norm_back(pkv[h, me, 0].astype(F32), sums[:, :dim])
        ag[h, me] = jnp.concatenate([dk, sums[:, dim:]], axis=1).astype(BF16)
        send_all(
            remote(
                lambda peer, h=h: ag.at[h, me], ag.at[h, me], ag_send.at[h], ag_recv.at[h]
            )
        )

    loads[-1].wait()
    half = kv_heads * dim
    piece = None
    for h in range(kv_heads):
        drain(ag.at[h], ag_recv.at[h])
        grads = ag[h].astype(F32).reshape(prompt, 2 * dim).astype(BF16)
        at = slice(h * dim, (h + 1) * dim)
        w_h = jnp.concatenate(
            [wv[:, at], wv[:, half + h * dim : half + (h + 1) * dim]], axis=1
        )
        part = dot_nt(grads, w_h)
        piece = part if piece is None else piece + part
    hs_src[...] = piece.reshape(n, per, piece.shape[1]).astype(BF16)
    send_all(remote(lambda peer: hs_src.at[peer], hs_dst.at[me], hs_send, hs_recv))
    hs_dst[me] = hs_src[me]

    def finish(h, _):
        drain(rs_src.at[h], rs_send.at[h])
        drain(pkv.at[h], pg_send.at[h])
        drain(ag.at[h], ag_send.at[h])
        return 0

    lax.fori_loop(0, kv_heads, finish, 0)
    drain(hs_src, hs_send)
    drain(hs_dst, hs_recv)
    ho_ref[...] = hs_dst[...]


def write_out(qo, ko, vo, ho, q_hbm, k_hbm, v_hbm, h_hbm, hidden, sem):
    copies = [
        pltpu.make_async_copy(src, dst, sem.at[i])
        for i, (src, dst) in enumerate(((qo, q_hbm), (ko, k_hbm), (vo, v_hbm), (hidden, h_hbm)))
    ]
    for copy in copies[:3]:
        copy.start()
    hidden[...] = jnp.concatenate(
        [ho[i].astype(F32) for i in range(ho.shape[0])], axis=1
    ).astype(BF16)
    copies[3].start()
    for copy in copies:
        copy.wait()


def solution(mesh):
    n = mesh.shape["cand"]

    def on_device(pk, pv, q, k, v, g, lengths, seen, gq, gk, w):
        dim = gq.shape[0]
        slots, q_width = q.shape
        kv_heads = k.shape[1] // dim
        group = q_width // (kv_heads * dim)
        wide = 2 if group % 2 == 0 else 1
        per = pk.shape[0]
        m = w.shape[0]
        prompt = n * per
        total = prompt + slots
        smem = pl.BlockSpec(memory_space=pltpu.SMEM)
        vmem = pl.BlockSpec(memory_space=pltpu.VMEM)
        anywhere = pl.BlockSpec(memory_space=pl.ANY)
        qo, ko, vo, ho = pl.pallas_call(
            functools.partial(kernel, n),
            out_shape=(
                pltpu.VMEM(q.shape, BF16),
                pltpu.VMEM(k.shape, BF16),
                pltpu.VMEM(v.shape, BF16),
                pltpu.VMEM((n, per, m), BF16),
            ),
            in_specs=[smem] * 2 + [pl.BlockSpec(memory_space=pltpu.HBM)] * 9,
            out_specs=(vmem,) * 4,
            scratch_shapes=[
                pltpu.VMEM(gq.shape, F32),
                pltpu.VMEM(gk.shape, F32),
                pltpu.VMEM((kv_heads, n, 2, per, dim), BF16),
                pltpu.VMEM(q.shape, BF16),
                pltpu.VMEM(k.shape, BF16),
                pltpu.VMEM(v.shape, BF16),
                pltpu.VMEM(g.shape, BF16),
                pltpu.VMEM(w.shape, BF16),
                pltpu.VMEM((total, wide * slots), F32),
                pltpu.VMEM((group // wide, prompt, wide * slots), F32),
                pltpu.VMEM((group // wide, prompt, wide * slots), F32),
                pltpu.VMEM((kv_heads, group // wide, slots, wide * slots), F32),
                pltpu.VMEM((kv_heads, group // wide, slots, wide * slots), F32),
                pltpu.VMEM((total, group * slots), BF16),
                pltpu.VMEM((kv_heads, 1, group * slots), F32),
                pltpu.VMEM((kv_heads, 2, 8, group * slots), F32),
                pltpu.VMEM((kv_heads, total, group * slots), BF16),
                pltpu.VMEM((kv_heads, dim, group * slots), F32),
                pltpu.VMEM((kv_heads, dim, total), BF16),
                pltpu.VMEM((kv_heads, slots, 2 * dim), F32),
                pltpu.VMEM((kv_heads, n, per, 2 * dim), BF16),
                pltpu.VMEM((kv_heads, n, per, 2 * dim), BF16),
                pltpu.VMEM((kv_heads, n, per, 2 * dim), BF16),
                pltpu.VMEM((n, per, m), BF16),
                pltpu.VMEM((n, per, m), BF16),
                pltpu.SemaphoreType.DMA((2, kv_heads)),
                pltpu.SemaphoreType.DMA((7,)),
            ]
            + [pltpu.SemaphoreType.DMA((kv_heads,))] * 6
            + [pltpu.SemaphoreType.DMA] * 2,
            compiler_params=pltpu.CompilerParams(
                collective_id=0,
                has_side_effects=True,
                vmem_limit_bytes=48 * 1024 * 1024,
            ),
        )(
            lengths,
            seen,
            *[
                pltpu.with_memory_space_constraint(x, pltpu.HBM)
                for x in (gq, gk, pk, pv, q, k, v, g, w)
            ],
        )
        return pl.pallas_call(
            write_out,
            out_shape=(
                jax.ShapeDtypeStruct(q.shape, BF16),
                jax.ShapeDtypeStruct(k.shape, BF16),
                jax.ShapeDtypeStruct(v.shape, BF16),
                jax.ShapeDtypeStruct((per, n * m), BF16),
            ),
            in_specs=[vmem] * 4,
            out_specs=(anywhere,) * 4,
            scratch_shapes=[
                pltpu.VMEM((per, n * m), BF16),
                pltpu.SemaphoreType.DMA((4,)),
            ],
            compiler_params=pltpu.CompilerParams(vmem_limit_bytes=8 * 1024 * 1024),
        )(*[pltpu.with_memory_space_constraint(x, pltpu.VMEM) for x in (qo, ko, vo, ho)])

    rows = P(("grp", "cand"), None)
    return jax.shard_map(
        on_device,
        mesh=mesh,
        in_specs=(rows,) * 6 + (P(("grp", "cand")), P(("grp", "cand")), P(), P(), P("cand", None)),
        out_specs=(rows,) * 4,
        check_vma=False,
    )
```

```python
import functools
import math

import jax
import jax.numpy as jnp
from jax import lax
from jax.experimental import pallas as pl
from jax.experimental.pallas import tpu as pltpu
from jax.sharding import PartitionSpec as P

EPS = 1e-06
F32 = jnp.float32
BF16 = jnp.bfloat16


def dot_nt(a, b):
    return lax.dot_general(a, b, (((1,), (1,)), ((), ())), preferred_element_type=F32)


def dot_nn(a, b):
    return lax.dot_general(a, b, (((1,), (0,)), ((), ())), preferred_element_type=F32)


def kernel(
    n,
    len_ref,
    seen_ref,
    gq_hbm,
    gk_hbm,
    pk_hbm,
    pv_hbm,
    q_hbm,
    k_hbm,
    v_hbm,
    g_hbm,
    w_hbm,
    qo,
    ko_ref,
    vo_ref,
    ho_ref,
    gq_ref,
    gk_ref,
    pkv,
    qv,
    kv,
    vv,
    gv,
    wv,
    mask,
    ev,
    dpv,
    er,
    dpr,
    pv,
    rv,
    sums_v,
    dsv,
    xcv,
    kgt,
    pr,
    stats,
    rs_src,
    rs_dst,
    ag,
    hs_src,
    hs_dst,
    own_sem,
    in_sem,
    pg_send,
    pg_recv,
    rs_send,
    rs_recv,
    ag_send,
    ag_recv,
    hs_send,
    hs_recv,
):
    me = lax.axis_index("cand")
    slots, q_width = qv.shape
    kv_heads = rs_src.shape[0]
    per = pkv.shape[3]
    dim = gq_ref.shape[0]
    prompt = n * per
    total = prompt + slots
    group = q_width // (kv_heads * dim)
    wide = 2 if group % 2 == 0 else 1
    pairs = group // wide
    lanes = wide * slots
    chunk = math.gcd(math.gcd(prompt, slots), 64)
    scale = dim ** (-0.5)

    own = [
        pltpu.make_async_copy(
            src.at[:, h * dim : (h + 1) * dim], pkv.at[h, me, i], own_sem.at[i, h]
        )
        for i, src in enumerate((pk_hbm, pv_hbm))
        for h in range(kv_heads)
    ]
    loads = [
        pltpu.make_async_copy(src, dst, in_sem.at[i])
        for i, (src, dst) in enumerate(
            (
                (gq_hbm, gq_ref),
                (gk_hbm, gk_ref),
                (k_hbm, kv),
                (v_hbm, vv),
                (q_hbm, qv),
                (g_hbm, gv),
                (w_hbm, wv),
            )
        )
    ]
    for copy in own:
        copy.start()

    barrier = pltpu.get_barrier_semaphore()

    def greet(step, _):
        peer = lax.rem(me + step, n)
        pl.semaphore_signal(
            barrier, inc=1, device_id={"cand": peer}, device_id_type=pl.DeviceIdType.MESH
        )
        return 0

    lax.fori_loop(1, n, greet, 0, unroll=n <= 16)
    for copy in loads[:-1]:
        copy.start()
    pl.semaphore_wait(barrier, n - 1)

    def send_all(copy_of):
        def body(step, _):
            copy_of(lax.rem(me + step, n)).start()
            return 0

        lax.fori_loop(1, n, body, 0, unroll=n <= 16)

    def remote(src, dst, send, recv):
        def copy_of(peer):
            return pltpu.make_async_remote_copy(
                src_ref=src(peer),
                dst_ref=dst,
                send_sem=send,
                recv_sem=recv,
                device_id={"cand": peer},
                device_id_type=pl.DeviceIdType.MESH,
            )

        return copy_of

    def drain(buffer, sem):
        part = buffer.at[pl.ds(0, n - 1)]
        pltpu.make_async_copy(part, part, sem).wait()

    for copy in own:
        copy.wait()
    for h in range(kv_heads):
        send_all(
            remote(
                lambda peer, h=h: pkv.at[h, me], pkv.at[h, me], pg_send.at[h], pg_recv.at[h]
            )
        )
    loads[-1].start()
    for copy in loads[:2]:
        copy.wait()

    gq = gq_ref[...].reshape(1, dim)
    gk = gk_ref[...].reshape(1, dim)
    both = gq * gk
    row = lax.broadcasted_iota(jnp.int32, (slots, dim), 0)
    live = (row < len_ref[0]).astype(F32).astype(BF16)
    key = lax.broadcasted_iota(jnp.int32, (prompt, slots), 0)
    seen = (key < seen_ref[0]).astype(F32)
    slot_j = lax.broadcasted_iota(jnp.int32, (slots, slots), 0)
    slot_i = lax.broadcasted_iota(jnp.int32, (slots, slots), 1)
    causal = (slot_j <= slot_i).astype(F32)
    for b in range(wide):
        mask[:prompt, b * slots : (b + 1) * slots] = seen
        mask[prompt:, b * slots : (b + 1) * slots] = causal
    eye_r = lax.broadcasted_iota(jnp.int32, (dim, dim), 0)
    eye_c = lax.broadcasted_iota(jnp.int32, (dim, dim), 1)
    eye = (eye_r == eye_c).astype(F32).astype(BF16)

    def head_lanes(head):
        return pl.ds(pl.multiple_of(head * dim, dim), dim)

    def key_factor(x):
        return lax.rsqrt(jnp.mean(x * x, axis=-1, keepdims=True) + EPS)

    for copy in loads[2:-1]:
        copy.wait()

    def load_heads(h):
        heads = [qv[:, head_lanes(h * group + a)] for a in range(group)]
        x_all = jnp.concatenate(heads, axis=0)
        heads = [gv[:, head_lanes(h * group + a)] * live for a in range(group)]
        return x_all, jnp.concatenate(heads, axis=0)

    def lift(h, at, e_ref, dp_ref, first, tops, inner):
        up = rv[h, :, at] * (scale * math.log2(math.e))
        for c in range(0, e_ref.shape[0], chunk):
            rows = slice(c, c + chunk)
            e = jnp.exp2(e_ref[rows] * up) * mask[first + c : first + c + chunk]
            e_ref[rows] = e
            tops = tops + jnp.sum(e.reshape(chunk // 8, 8, lanes), axis=0)
            inner = inner + jnp.sum(
                (e * dp_ref[rows]).reshape(chunk // 8, 8, lanes), axis=0
            )
        return tops, inner

    def respond(h, _):
        raw = kv[:, head_lanes(h)].astype(F32)
        kg32 = raw * key_factor(raw) * both
        kgt[h, :, prompt:] = kg32.T.astype(BF16)
        left = jnp.concatenate([kg32.astype(BF16), eye], axis=0)
        val = vv[:, head_lanes(h)]
        x_all, g_all = load_heads(h)
        for b in range(pairs):
            at = slice(b * lanes, (b + 1) * lanes)
            both_t = dot_nt(left, x_all[at])
            er[h, b] = both_t[:slots]
            x_t = both_t[slots:]
            r = lax.rsqrt(jnp.mean(x_t * x_t, axis=0, keepdims=True) + EPS)
            rv[h, :, at] = r
            xcv[h, :, at] = x_t * r
            dpr[h, b] = dot_nt(val, g_all[at])
            zero = jnp.zeros((8, lanes), F32)
            tops, inner = lift(h, at, er.at[h, b], dpr.at[h, b], prompt, zero, zero)
            sums_v[h, 0, :, at] = tops
            sums_v[h, 1, :, at] = inner
        return 0

    lax.fori_loop(0, kv_heads, respond, 0)

    def forward(h, _):
        drain(pkv.at[h], pg_recv.at[h])
        raw = pkv[h, :, 0].astype(F32).reshape(prompt, dim)
        kg32 = raw * key_factor(raw) * both
        kgt[h, :, :prompt] = kg32.T.astype(BF16)
        left = kg32.astype(BF16)
        val = pkv[h, :, 1].astype(F32).reshape(prompt, dim).astype(BF16)
        x_all, g_all = load_heads(h)
        for b in range(pairs):
            at = slice(b * lanes, (b + 1) * lanes)
            ev[b] = dot_nt(left, x_all[at])
            dpv[b] = dot_nt(val, g_all[at])
            tops, inner = lift(
                h, at, ev.at[b], dpv.at[b], 0, sums_v[h, 0, :, at], sums_v[h, 1, :, at]
            )
            inv = 1.0 / jnp.sum(tops, axis=0, keepdims=True)
            delta = jnp.sum(inner, axis=0, keepdims=True) * inv
            down = inv * (rv[h, :, at] * scale)
            for i, value in enumerate((inv, delta, down)):
                stats[h, i, :, at] = value
            for c in range(0, prompt, chunk):
                rows = slice(c, c + chunk)
                e = ev[b, rows]
                pv[rows, at] = (e * inv).astype(BF16)
                dsv[h, rows, at] = (e * (dpv[b, rows] - delta) * down).astype(BF16)
        dv = dot_nn(pv[...], g_all)
        dk = dot_nn(dsv[h, :prompt], x_all)
        rs_src[h, :, :, :dim] = dk.reshape(n, per, dim).astype(BF16)
        rs_src[h, :, :, dim:] = dv.reshape(n, per, dim).astype(BF16)
        send_all(
            remote(
                lambda peer: rs_src.at[h, peer],
                rs_dst.at[h, me],
                rs_send.at[h],
                rs_recv.at[h],
            )
        )
        rs_dst[h, me] = rs_src[h, me]
        return 0

    lax.fori_loop(0, kv_heads, forward, 0)

    def norm_back(x, upstream):
        r = key_factor(x)
        w = upstream * both
        inner = jnp.mean(w * x, axis=-1, keepdims=True)
        return r * w - x * (r * r * r) * inner

    def query_side(h, _):
        x_all, g_all = load_heads(h)
        for b in range(pairs):
            at = slice(b * lanes, (b + 1) * lanes)
            inv, delta, down = [stats[h, i, :, at] for i in range(3)]
            for c in range(0, slots, chunk):
                rows = slice(c, c + chunk)
                e = er[h, b, rows]
                pr[rows, at] = (e * inv).astype(BF16)
                dsv[h, prompt + c : prompt + c + chunk, at] = (
                    e * (dpr[h, b, rows] - delta) * down
                ).astype(BF16)
            dq = dot_nn(kgt[h], dsv[h, :, at])
            x_t = xcv[h, :, at]
            dx = dq - x_t * jnp.mean(dq * x_t, axis=0, keepdims=True)
            for a in range(wide):
                head = h * group + b * wide + a
                qo[:, head_lanes(head)] = dx[:, a * slots : (a + 1) * slots].T.astype(BF16)
        dk = dot_nn(dsv[h, prompt:], x_all)
        at = head_lanes(h)
        ko_ref[:, at] = norm_back(kv[:, at].astype(F32), dk).astype(BF16)
        vo_ref[:, at] = dot_nn(pr[...], g_all).astype(BF16)
        return 0

    lax.fori_loop(0, kv_heads, query_side, 0)

    for h in range(kv_heads):
        drain(rs_dst.at[h], rs_recv.at[h])
        sums = jnp.sum(rs_dst[h].astype(F32), axis=0)
        dk = norm_back(pkv[h, me, 0].astype(F32), sums[:, :dim])
        ag[h, me] = jnp.concatenate([dk, sums[:, dim:]], axis=1).astype(BF16)
        send_all(
            remote(
                lambda peer, h=h: ag.at[h, me], ag.at[h, me], ag_send.at[h], ag_recv.at[h]
            )
        )

    loads[-1].wait()
    half = kv_heads * dim
    piece = None
    for h in range(kv_heads):
        drain(ag.at[h], ag_recv.at[h])
        grads = ag[h].astype(F32).reshape(prompt, 2 * dim).astype(BF16)
        at = slice(h * dim, (h + 1) * dim)
        w_h = jnp.concatenate(
            [wv[:, at], wv[:, half + h * dim : half + (h + 1) * dim]], axis=1
        )
        part = dot_nt(grads, w_h)
        piece = part if piece is None else piece + part
    hs_src[...] = piece.reshape(n, per, piece.shape[1]).astype(BF16)
    send_all(remote(lambda peer: hs_src.at[peer], hs_dst.at[me], hs_send, hs_recv))
    hs_dst[me] = hs_src[me]

    def finish(h, _):
        drain(rs_src.at[h], rs_send.at[h])
        drain(pkv.at[h], pg_send.at[h])
        drain(ag.at[h], ag_send.at[h])
        return 0

    lax.fori_loop(0, kv_heads, finish, 0)
    drain(hs_src, hs_send)
    drain(hs_dst, hs_recv)
    ho_ref[...] = hs_dst[...]


def write_out(qo, ko, vo, ho, q_hbm, k_hbm, v_hbm, h_hbm, hidden, sem):
    copies = [
        pltpu.make_async_copy(src, dst, sem.at[i])
        for i, (src, dst) in enumerate(((qo, q_hbm), (ko, k_hbm), (vo, v_hbm), (hidden, h_hbm)))
    ]
    for copy in copies[:3]:
        copy.start()
    hidden[...] = jnp.concatenate(
        [ho[i].astype(F32) for i in range(ho.shape[0])], axis=1
    ).astype(BF16)
    copies[3].start()
    for copy in copies:
        copy.wait()


def solution(mesh):
    n = mesh.shape["cand"]

    def on_device(pk, pv, q, k, v, g, lengths, seen, gq, gk, w):
        dim = gq.shape[0]
        slots, q_width = q.shape
        kv_heads = k.shape[1] // dim
        group = q_width // (kv_heads * dim)
        wide = 2 if group % 2 == 0 else 1
        per = pk.shape[0]
        m = w.shape[0]
        prompt = n * per
        total = prompt + slots
        smem = pl.BlockSpec(memory_space=pltpu.SMEM)
        vmem = pl.BlockSpec(memory_space=pltpu.VMEM)
        anywhere = pl.BlockSpec(memory_space=pl.ANY)
        qo, ko, vo, ho = pl.pallas_call(
            functools.partial(kernel, n),
            out_shape=(
                pltpu.VMEM(q.shape, BF16),
                pltpu.VMEM(k.shape, BF16),
                pltpu.VMEM(v.shape, BF16),
                pltpu.VMEM((n, per, m), BF16),
            ),
            in_specs=[smem] * 2 + [pl.BlockSpec(memory_space=pltpu.HBM)] * 9,
            out_specs=(vmem,) * 4,
            scratch_shapes=[
                pltpu.VMEM(gq.shape, F32),
                pltpu.VMEM(gk.shape, F32),
                pltpu.VMEM((kv_heads, n, 2, per, dim), BF16),
                pltpu.VMEM(q.shape, BF16),
                pltpu.VMEM(k.shape, BF16),
                pltpu.VMEM(v.shape, BF16),
                pltpu.VMEM(g.shape, BF16),
                pltpu.VMEM(w.shape, BF16),
                pltpu.VMEM((total, wide * slots), F32),
                pltpu.VMEM((group // wide, prompt, wide * slots), F32),
                pltpu.VMEM((group // wide, prompt, wide * slots), F32),
                pltpu.VMEM((kv_heads, group // wide, slots, wide * slots), F32),
                pltpu.VMEM((kv_heads, group // wide, slots, wide * slots), F32),
                pltpu.VMEM((prompt, group * slots), BF16),
                pltpu.VMEM((kv_heads, 1, group * slots), F32),
                pltpu.VMEM((kv_heads, 2, 8, group * slots), F32),
                pltpu.VMEM((kv_heads, total, group * slots), BF16),
                pltpu.VMEM((kv_heads, dim, group * slots), F32),
                pltpu.VMEM((kv_heads, dim, total), BF16),
                pltpu.VMEM((slots, group * slots), BF16),
                pltpu.VMEM((kv_heads, 3, 1, group * slots), F32),
                pltpu.VMEM((kv_heads, n, per, 2 * dim), BF16),
                pltpu.VMEM((kv_heads, n, per, 2 * dim), BF16),
                pltpu.VMEM((kv_heads, n, per, 2 * dim), BF16),
                pltpu.VMEM((n, per, m), BF16),
                pltpu.VMEM((n, per, m), BF16),
                pltpu.SemaphoreType.DMA((2, kv_heads)),
                pltpu.SemaphoreType.DMA((7,)),
            ]
            + [pltpu.SemaphoreType.DMA((kv_heads,))] * 6
            + [pltpu.SemaphoreType.DMA] * 2,
            compiler_params=pltpu.CompilerParams(
                collective_id=0,
                has_side_effects=True,
                vmem_limit_bytes=48 * 1024 * 1024,
            ),
        )(
            lengths,
            seen,
            *[
                pltpu.with_memory_space_constraint(x, pltpu.HBM)
                for x in (gq, gk, pk, pv, q, k, v, g, w)
            ],
        )
        return pl.pallas_call(
            write_out,
            out_shape=(
                jax.ShapeDtypeStruct(q.shape, BF16),
                jax.ShapeDtypeStruct(k.shape, BF16),
                jax.ShapeDtypeStruct(v.shape, BF16),
                jax.ShapeDtypeStruct((per, n * m), BF16),
            ),
            in_specs=[vmem] * 4,
            out_specs=(anywhere,) * 4,
            scratch_shapes=[
                pltpu.VMEM((per, n * m), BF16),
                pltpu.SemaphoreType.DMA((4,)),
            ],
            compiler_params=pltpu.CompilerParams(vmem_limit_bytes=8 * 1024 * 1024),
        )(*[pltpu.with_memory_space_constraint(x, pltpu.VMEM) for x in (qo, ko, vo, ho)])

    rows = P(("grp", "cand"), None)
    return jax.shard_map(
        on_device,
        mesh=mesh,
        in_specs=(rows,) * 6 + (P(("grp", "cand")), P(("grp", "cand")), P(), P(), P("cand", None)),
        out_specs=(rows,) * 4,
        check_vma=False,
    )
```
